32 devices in a mesh: group: 2 (over x), freq: 16 (over z, y, core).
Axes of the slice: x: 2, y: 2, z: 4, core: 2. Of those that a mesh axis runs over, the one named last changes fastest.
Arguments:
- traces: bfloat16 [512, 256, 256], P(('group', 'freq')), parts along dimension 0, may hold values from -6 to 6
- velocity: bfloat16 [32, 256, 256], P(('group', 'freq')), parts along dimension 0, may hold values from 1 to 2
- poly_coef: float32 [2, 10, 4], replicated, may hold values from -0.6 to 0.6
- freq_slot: int32 [16], replicated, may hold values from 0 to 15, each once
- depth_owner: int32 [8], P('group'), parts along dimension 0, may hold values from 0 to 15, as said below
Outputs:
- depth_image: float32 [4, 512, 256], P(None, ('group', 'freq')), parts along dimension 1
- wavefield: float32 [2, 32, 256, 256], P(None, ('group', 'freq')), parts along dimension 1
The draws below stay inside these ranges and needn't reach their ends.
There are 2 independent parts, one for each index of `group`. The reference program is written for one: setup_inputs(seed, part) draws one part's arguments, and reference() takes and returns one part's arrays. A program takes and returns all parts, laid end to end along the dimension named above; an argument that names none is the same for every part. Nothing has to cross between parts.
Inputs may be any that keep to these rules, and one draw needn't show every extreme that they name: `freq_slot`: each slot holds a different frequency index. `depth_owner`: the 4 entries are different.
All inputs are finite; a program needn't handle non-finite values.
Results may differ from the reference program's by a relative error of at most 0.0023.
Values may be sent and summed in bfloat16 or wider, within the bound.
A program may use at most 128 MiB of HBM per device.

```python
import math
import jax
import jax.numpy as jnp
from jax import lax

NX = 256
NY = 256
NT = 256
NTERM = 10
NPOW = 4
NZ = 4
NF = 16
VSLICES = 16


def draw_depth_owner(key, part):
    middle_owners = jax.random.permutation(jax.random.fold_in(key, 11), VSLICES - 2)[:NZ - 2] + 1
    chosen = jnp.concatenate([jnp.array([0, VSLICES - 1], jnp.int32), middle_owners.astype(jnp.int32)])
    shuffle = jax.random.permutation(jax.random.fold_in(key, 12), NZ)
    return chosen[shuffle].astype(jnp.int32)


def shard_levels(rng, shape, pieces, low, top_value):
    factor_of, own = 1.0, jax.random.fold_in(rng, 6)
    for position, parts in pieces:
        draws = jnp.exp(jax.random.uniform(jax.random.fold_in(own, position), (parts,), jnp.float32, low / len(pieces), top_value / len(pieces)))
        factor_of = factor_of * jnp.repeat(draws, shape[position] // parts).reshape([-1 if axis == position else 1 for axis in range(len(shape))])
    return factor_of


def gaussian(stream_key, extent, width, most, pieces=(), kind=jnp.bfloat16):
    entries = jax.random.normal(stream_key, extent, jnp.float32) * width
    if len(pieces) > 0:
        entries = shard_levels(stream_key, extent, pieces, -0.22, 0.18) * entries
    return jnp.clip(entries, min=-most, max=most).astype(kind)


def setup_inputs(seed: int = 0, part: int = 0) -> dict:
    arg_keys = jax.random.split(jax.random.key(seed), 6)
    part_keys = jax.random.split(jax.random.fold_in(arg_keys[5], part), 6)
    traces = gaussian(part_keys[0], (NX, NY, NT), 1.0, 6.0, ((0, 16),))
    velocity = jnp.clip(1.0 + 1.0 * jax.random.uniform(part_keys[1], (VSLICES, NX, NY), jnp.float32) ** shard_levels(part_keys[1], (VSLICES, NX, NY), ((0, 16),), -0.2, 0.2), 1.0, 2.0).astype(jnp.bfloat16)
    poly_coef = gaussian(arg_keys[2], (2, NTERM, NPOW), 0.1, 0.6, (), jnp.float32)
    freq_slot = jax.random.permutation(arg_keys[3], NF).astype(jnp.int32)
    depth_owner = draw_depth_owner(jax.random.fold_in(jax.random.fold_in(arg_keys[5], part), 71), part)
    return {"traces": traces, "velocity": velocity, "poly_coef": poly_coef, "freq_slot": freq_slot, "depth_owner": depth_owner}


def mcclellan(values):
    padded = jnp.pad(values, [(0, 0)] * (values.ndim - 2) + [(1, 1), (1, 1)])
    row_sum = padded[..., :-2, :] + 2.0 * padded[..., 1:-1, :] + padded[..., 2:, :]
    smoothed = row_sum[..., :-2] + 2.0 * row_sum[..., 1:-1] + row_sum[..., 2:]
    return smoothed * 0.125 - values

def coefficient_pair(poly_coef, order_index, powers):
    real_part = poly_coef[0, order_index, 0] * powers[0]
    imag_part = poly_coef[1, order_index, 0] * powers[0]
    for power_index in range(1, len(powers)):
        real_part = real_part + poly_coef[0, order_index, power_index] * powers[power_index]
        imag_part = imag_part + poly_coef[1, order_index, power_index] * powers[power_index]
    return (real_part, imag_part)

def accumulate(summed, real_part, imag_part, term):
    new_real = summed[0] + real_part * term[0] - imag_part * term[1]
    new_imag = summed[1] + real_part * term[1] + imag_part * term[0]
    return jnp.stack([new_real, new_imag])

def reference(traces, velocity, poly_coef, freq_slot, depth_owner):
    freq_bin = (freq_slot + 1).astype(jnp.int32)
    sample_index = jnp.arange(NT, dtype=jnp.int32)
    phase_int = freq_bin[:, None] * sample_index[None, :] % NT
    phases = phase_int.astype(jnp.float32) * (2.0 * math.pi / NT)
    dft_table = (jnp.stack([jnp.cos(phases), -jnp.sin(phases)]) / math.sqrt(NT)).astype(jnp.bfloat16)
    wavefield = jnp.einsum('cft,xyt->cfxy', dft_table.astype(jnp.float32), traces.astype(jnp.float32), precision=lax.Precision.HIGHEST)
    freq_value = freq_bin.astype(jnp.float32)
    image_terms = []
    for depth_index in range(NZ):
        speed = velocity[depth_owner[depth_index]].astype(jnp.float32)
        slowness = freq_value[:, None, None] / (NF * speed[None, :, :])
        powers = [jnp.ones_like(slowness)]
        for power_index in range(1, NPOW):
            powers.append(powers[-1] * slowness)
        term_prev = wavefield
        real_part, imag_part = coefficient_pair(poly_coef, 0, powers)
        summed = accumulate(jnp.zeros_like(wavefield), real_part, imag_part, term_prev)
        term_now = mcclellan(wavefield)
        real_part, imag_part = coefficient_pair(poly_coef, 1, powers)
        summed = accumulate(summed, real_part, imag_part, term_now)
        for order_index in range(2, NTERM):
            term_next = 2.0 * mcclellan(term_now) - term_prev
            real_part, imag_part = coefficient_pair(poly_coef, order_index, powers)
            summed = accumulate(summed, real_part, imag_part, term_next)
            term_prev, term_now = (term_now, term_next)
        wavefield = summed
        image_terms.append(lax.optimization_barrier(jnp.sum(wavefield[0], axis=0)) / math.sqrt(NF))
    return (jnp.stack(image_terms), wavefield)
```

```python
import functools
import math

import jax
import jax.numpy as jnp
import numpy as np
from jax import lax
from jax.experimental import pallas as pl
from jax.experimental.pallas import tpu as pltpu
from jax.sharding import PartitionSpec as P

F32, BF16 = jnp.float32, jnp.bfloat16


def sine_basis(size):
    index = np.arange(1, size + 1, dtype=np.float64)
    basis = math.sqrt(2.0 / (size + 1)) * np.sin(np.pi * np.outer(index, index) / (size + 1))
    return basis, 2.0 + 2.0 * np.cos(np.pi * index / (size + 1))


def split(values):
    high = values.astype(BF16)
    return high, (values - high.astype(F32)).astype(BF16)


def np_split(values):
    high = values.astype(BF16)
    return np.stack([high, (values - high.astype(np.float64)).astype(BF16)])


def dot(a, b):
    return lax.dot_general(a, b, (((1,), (0,)), ((), ())), preferred_element_type=F32)


def right(values, basis):
    high, low = split(values)
    return dot(high, basis[0]) + dot(low, basis[0]) + dot(high, basis[1])


def left(basis, values):
    high, low = split(values)
    return dot(basis[0], high) + dot(basis[0], low) + dot(basis[1], high)


def kernel(n, poly, owner, slot, spec, vel, lam, sx, sy, image, field,
           precv, vrecv, vsel, vall, poles, hat, slow, mine, theirs, part, irecv,
           p_send, p_recv, w_send, w_recv, a_send, f_send, a_recv, x_send, x_recv, i_send, i_recv):
    me = lax.axis_index("freq")
    core = lax.rem(me, 2)
    partner = me + 1 - 2 * core
    half = n // 2
    rows = spec.shape[2]
    nx, ny = field.shape[1:]
    depth_count = image.shape[0]
    term_count, power_count = poly.shape[1], poly.shape[2]

    def copy(src, dst, ssem, rsem, peer):
        return pltpu.make_async_remote_copy(
            src_ref=src, dst_ref=dst, send_sem=ssem, recv_sem=rsem,
            device_id={"freq": peer}, device_id_type=pl.DeviceIdType.MESH)

    def peers(count, step, body):
        @pl.loop(1, count)
        def _(k):
            body(lax.rem(me + step * k, n))

    barrier = pltpu.get_barrier_semaphore()
    peers(n, 1, lambda p: pl.semaphore_signal(
        barrier, inc=1, device_id={"freq": p}, device_id_type=pl.DeviceIdType.MESH))
    pl.semaphore_wait(barrier, n - 1)

    def v_copy(p, block, slot_of):
        return copy(vel.at[block], vrecv.at[slot_of], w_send.at[p], w_recv.at[slot_of], p)

    def p_copy(p, block, slot_of):
        return copy(spec.at[block], precv.at[slot_of], p_send.at[p], p_recv.at[slot_of], p)

    peers(n, 1, lambda p: v_copy(p, p, me).start())
    peers(n, 1, lambda p: p_copy(p, p, me).start())
    vrecv[me] = vel[me]
    precv[me] = spec[me]

    chunk = 16 if nx % 16 == 0 else nx

    @pl.loop(0, nx // chunk)
    def _(c):
        at = pl.ds(pl.multiple_of(c * chunk, chunk), chunk)
        x = lam[at, :]
        before, now = jnp.ones_like(x), x
        sums = [[jnp.full_like(x, poly[part_, 0, j]) + poly[part_, 1, j] * x for j in range(power_count)]
                for part_ in range(2)]
        for k in range(2, term_count):
            before, now = now, 2.0 * (x * now) - before
            for part_ in range(2):
                for j in range(power_count):
                    sums[part_][j] = sums[part_][j] + poly[part_, k, j] * now
        for part_ in range(2):
            for j in range(power_count):
                poles[j, part_, at, :] = sums[part_][j]

    peers(n, 1, lambda p: v_copy(p, p, p).wait_recv())
    for z in range(depth_count):
        vsel[z] = vrecv[owner[z]]
    vall[me] = vsel[...]

    def a_copy(p, slot_of):
        return copy(vsel, vall.at[slot_of], a_send.at[p], a_recv.at[slot_of], p)

    def f_copy(block):
        return copy(vall.at[block], vall.at[block], f_send.at[block], a_recv.at[block], partner)

    peers(half, 2, lambda p: a_copy(p, me).start())
    copy(vsel, vall.at[me], f_send.at[me], a_recv.at[me], partner).start()

    peers(n, 1, lambda p: p_copy(p, p, p).wait_recv())
    for d in range(n):
        for c in range(2):
            field[c, d * rows:(d + 1) * rows, :] = precv[d, c].astype(F32)

    def gather_velocity():
        def forward(p):
            a_copy(p, p).wait_recv()
            f_copy(p).start()

        peers(half, 2, forward)

        @pl.loop(0, half)
        def _(k):
            block = lax.rem(partner + 2 * k, n)
            copy(vsel, vall.at[block], f_send.at[block], a_recv.at[block], partner).wait_recv()

    bin_value = (slot[me] + 1).astype(F32) * (1.0 / n)

    def x_copy(z):
        return copy(mine.at[z, 1 - core], theirs.at[z], x_send.at[z], x_recv.at[z], partner)

    def i_copy(z, p, slot_of):
        return copy(part.at[z, lax.div(p, 2)], irecv.at[z, slot_of],
                    i_send.at[z, lax.div(p, 2)], i_recv.at[z, slot_of], p)

    def pass_on(z):
        x_copy(z).wait_recv()
        part[z] = mine[z, core] + theirs[z]
        peers(half, 2, lambda p: i_copy(z, p, lax.div(me, 2)).start())

    sxh, sxl, syh, syl = sx[0], sx[1], sy[0], sy[1]
    basis_x, basis_y = (sxh, sxl), (syh, syl)

    @pl.loop(0, depth_count)
    def _(z):
        for c in range(2):
            hat[c] = left(basis_x, right(field[c], basis_y))

        @pl.when(z == 0)
        def _():
            gather_velocity()

        @pl.when(z > 0)
        def _():
            pass_on(z - 1)

        for d in range(n):
            slow[d * rows:(d + 1) * rows, :] = bin_value / vall[d, z].astype(F32)

        field[...] = jnp.zeros_like(field)

        @pl.loop(0, power_count)
        def _(step):
            j = power_count - 1 - step
            for c in range(2):
                if c == 0:
                    scaled = poles[j, 0] * hat[0] - poles[j, 1] * hat[1]
                else:
                    scaled = poles[j, 0] * hat[1] + poles[j, 1] * hat[0]
                field[c] = field[c] * slow[...] + right(left(basis_x, scaled), basis_y)

        for d in range(n):
            mine[z, d % 2, d // 2] = field[0, d * rows:(d + 1) * rows, :]
        x_copy(z).start()

    pass_on(depth_count - 1)

    scale = 1.0 / math.sqrt(n)

    @pl.loop(0, depth_count)
    def _(z):
        irecv[z, lax.div(me, 2)] = part[z, lax.div(me, 2)]
        peers(half, 2, lambda p: i_copy(z, p, lax.div(p, 2)).wait_recv())
        total = irecv[z, 0]
        for i in range(1, half):
            total = total + irecv[z, i]
        image[z] = total * scale

    peers(n, 1, lambda p: v_copy(p, p, me).wait_send())
    peers(n, 1, lambda p: p_copy(p, p, me).wait_send())
    peers(half, 2, lambda p: a_copy(p, me).wait_send())
    copy(vsel, vall.at[me], f_send.at[me], a_recv.at[me], partner).wait_send()
    peers(half, 2, lambda p: f_copy(p).wait_send())

    @pl.loop(0, depth_count)
    def _(z):
        x_copy(z).wait_send()
        peers(half, 2, lambda p: i_copy(z, p, lax.div(me, 2)).wait_send())


def on_device(n, traces, velocity, poly_coef, freq_slot, depth_owner):
    rows, ny, sample_count = traces.shape
    nx = velocity.shape[1]
    depth_count = depth_owner.shape[0]
    power_count = poly_coef.shape[2]
    assert freq_slot.shape[0] == n and velocity.shape[0] == 1 and n % 2 == 0
    sample_index = jnp.arange(sample_count, dtype=jnp.int32)
    phase_int = (freq_slot + 1)[:, None] * sample_index[None, :] % sample_count
    phases = phase_int.astype(F32) * (2.0 * math.pi / sample_count)
    dft_table = (jnp.stack([jnp.cos(phases), -jnp.sin(phases)]) / math.sqrt(sample_count)).astype(BF16)
    spectra = jnp.einsum("cft,xyt->fcxy", dft_table, traces, preferred_element_type=F32).astype(BF16)

    basis_x, eig_x = sine_basis(nx)
    basis_y, eig_y = sine_basis(ny)
    lam = jnp.asarray((np.outer(eig_x, eig_y) / 8.0 - 1.0).astype(np.float32))
    vmem = pl.BlockSpec(memory_space=pltpu.VMEM)
    smem = pl.BlockSpec(memory_space=pltpu.SMEM)
    half = n // 2
    dma = pltpu.SemaphoreType.DMA
    return pl.pallas_call(
        functools.partial(kernel, n),
        out_shape=(jax.ShapeDtypeStruct((depth_count, rows, ny), F32),
                   jax.ShapeDtypeStruct((2, nx, ny), F32)),
        in_specs=[smem, smem, smem] + [vmem] * 5,
        out_specs=(vmem, vmem),
        scratch_shapes=[
            pltpu.VMEM((n, 2, rows, ny), BF16),
            pltpu.VMEM((n, rows, ny), BF16),
            pltpu.VMEM((depth_count, rows, ny), BF16),
            pltpu.VMEM((n, depth_count, rows, ny), BF16),
            pltpu.VMEM((power_count, 2, nx, ny), F32),
            pltpu.VMEM((2, nx, ny), F32),
            pltpu.VMEM((nx, ny), F32),
            pltpu.VMEM((depth_count, 2, half, rows, ny), F32),
            pltpu.VMEM((depth_count, half, rows, ny), F32),
            pltpu.VMEM((depth_count, half, rows, ny), F32),
            pltpu.VMEM((depth_count, half, rows, ny), F32),
            dma((n,)), dma((n,)), dma((n,)), dma((n,)), dma((n,)), dma((n,)), dma((n,)),
            dma((depth_count,)), dma((depth_count,)),
            dma((depth_count, half)), dma((depth_count, half)),
        ],
        compiler_params=pltpu.CompilerParams(collective_id=0, has_side_effects=True),
    )(poly_coef, depth_owner, freq_slot, spectra, velocity.reshape(n, rows, ny), lam,
      jnp.asarray(np_split(basis_x)), jnp.asarray(np_split(basis_y)))


def solution(mesh):
    def step(*args):
        depth_image, wavefield = on_device(mesh.shape["freq"], *args)
        return depth_image, wavefield[:, None]

    return jax.shard_map(
        step,
        mesh=mesh,
        in_specs=(
            P(("group", "freq"), None, None),
            P(("group", "freq"), None, None),
            P(),
            P(),
            P("group"),
        ),
        out_specs=(P(None, ("group", "freq"), None), P(None, ("group", "freq"), None, None)),
        check_vma=False,
    )
```

```python
import functools
import math

import jax
import jax.numpy as jnp
import numpy as np
from jax import lax
from jax.experimental import pallas as pl
from jax.experimental.pallas import tpu as pltpu
from jax.sharding import PartitionSpec as P

F32, BF16 = jnp.float32, jnp.bfloat16


def sine_basis(size):
    index = np.arange(1, size + 1, dtype=np.float64)
    basis = math.sqrt(2.0 / (size + 1)) * np.sin(np.pi * np.outer(index, index) / (size + 1))
    return basis, 2.0 + 2.0 * np.cos(np.pi * index / (size + 1))


def split(values):
    high = values.astype(BF16)
    return high, (values - high.astype(F32)).astype(BF16)


def np_split(values):
    high = values.astype(BF16)
    return np.stack([high, (values - high.astype(np.float64)).astype(BF16)])


def dot(a, b):
    return lax.dot_general(a, b, (((1,), (0,)), ((), ())), preferred_element_type=F32)


def right(values, basis):
    high, low = split(values)
    return dot(high, basis[0]) + dot(low, basis[0]) + dot(high, basis[1])


def left(basis, values):
    high, low = split(values)
    return dot(basis[0], high) + dot(basis[0], low) + dot(basis[1], high)


def kernel(n, poly, owner, slot, spec, vel, lam, sx, sy, image, field,
           precv, vrecv, vsel, vall, poles, hat, slow, mine, theirs, part, irecv,
           p_send, p_recv, w_send, w_recv, a_send, f_send, a_recv, g_send, x_send, x_recv, i_send, i_recv):
    me = lax.axis_index("freq")
    core = lax.rem(me, 2)
    partner = me + 1 - 2 * core
    half, line = n // 2, n // 4
    across = me + 2 - 4 * lax.rem(lax.div(me, 2), 2)
    rows = spec.shape[2]
    nx, ny = field.shape[1:]
    depth_count = image.shape[0]
    power_count, term_count = poly.shape[1], poly.shape[2]

    def copy(src, dst, ssem, rsem, peer):
        return pltpu.make_async_remote_copy(
            src_ref=src, dst_ref=dst, send_sem=ssem, recv_sem=rsem,
            device_id={"freq": peer}, device_id_type=pl.DeviceIdType.MESH)

    def peers(count, step, body):
        @pl.loop(1, count)
        def _(k):
            body(lax.rem(me + step * k, n))

    barrier = pltpu.get_barrier_semaphore()
    peers(n, 1, lambda p: pl.semaphore_signal(
        barrier, inc=1, device_id={"freq": p}, device_id_type=pl.DeviceIdType.MESH))
    pl.semaphore_wait(barrier, n - 1)

    def v_copy(p, block, slot_of):
        return copy(vel.at[block], vrecv.at[slot_of], w_send.at[p], w_recv.at[slot_of], p)

    def p_copy(p, block, slot_of):
        return copy(spec.at[block], precv.at[slot_of], p_send.at[p], p_recv.at[slot_of], p)

    peers(n, 1, lambda p: v_copy(p, p, me).start())
    peers(n, 1, lambda p: p_copy(p, p, me).start())
    vrecv[me] = vel[me]
    precv[me] = spec[me]

    chunk = 16 if nx % 16 == 0 else nx

    @pl.loop(0, nx // chunk)
    def _(c):
        at = pl.ds(pl.multiple_of(c * chunk, chunk), chunk)
        x = lam[at, :]
        before, now = jnp.ones_like(x), x
        sums = [[jnp.full_like(x, poly[part_, j, 0]) + poly[part_, j, 1] * x for j in range(power_count)]
                for part_ in range(2)]
        for k in range(2, term_count):
            before, now = now, 2.0 * (x * now) - before
            for part_ in range(2):
                for j in range(power_count):
                    sums[part_][j] = sums[part_][j] + poly[part_, j, k] * now
        for part_ in range(2):
            for j in range(power_count):
                poles[j, part_, at, :] = sums[part_][j]

    peers(n, 1, lambda p: v_copy(p, p, p).wait_recv())
    for z in range(depth_count):
        vsel[z] = vrecv[owner[z]]
    vall[me] = vsel[...]

    def a_copy(p, slot_of):
        return copy(vsel, vall.at[slot_of], a_send.at[p], a_recv.at[slot_of], p)

    def forward(src, block):
        return (copy(src, vall.at[block], g_send.at[block], a_recv.at[block], across),
                copy(src, vall.at[block], f_send.at[block], a_recv.at[block], partner))

    peers(line, 4, lambda p: a_copy(p, me).start())
    for send in forward(vsel, me):
        send.start()

    peers(n, 1, lambda p: p_copy(p, p, p).wait_recv())
    for d in range(n):
        for c in range(2):
            field[c, d * rows:(d + 1) * rows, :] = precv[d, c].astype(F32)

    def forward_line():
        def body(p):
            a_copy(p, p).wait_recv()
            for send in forward(vall.at[p], p):
                send.start()

        peers(line, 4, body)

    def forward_across():
        @pl.loop(0, line)
        def _(k):
            block = lax.rem(across + 4 * k, n)
            a_copy(block, block).wait_recv()
            forward(vall.at[block], block)[1].start()

    def wait_partner():
        @pl.loop(0, half)
        def _(k):
            block = lax.rem(partner + 2 * k, n)
            a_copy(block, block).wait_recv()

    bin_value = (slot[me] + 1).astype(F32) * (1.0 / n)

    def x_copy(z):
        return copy(mine.at[z, 1 - core], theirs.at[z], x_send.at[z], x_recv.at[z], partner)

    def i_copy(z, p, slot_of):
        return copy(part.at[z, lax.div(p, 2)], irecv.at[z, slot_of],
                    i_send.at[z, lax.div(p, 2)], i_recv.at[z, slot_of], p)

    def pass_on(z):
        x_copy(z).wait_recv()
        part[z] = mine[z, core] + theirs[z]
        peers(half, 2, lambda p: i_copy(z, p, lax.div(me, 2)).start())

    sxh, sxl, syh, syl = sx[0], sx[1], sy[0], sy[1]
    basis_x, basis_y = (sxh, sxl), (syh, syl)

    def beside(blocks):
        return jnp.concatenate(blocks, axis=1)

    def below(values, count):
        width = values.shape[1] // count
        return jnp.concatenate([values[:, i * width:(i + 1) * width] for i in range(count)], axis=0)

    def terms(c):
        scaled = []
        for j in range(power_count):
            if c == 0:
                scaled.append(poles[j, 0] * hat[0] - poles[j, 1] * hat[1])
            else:
                scaled.append(poles[j, 0] * hat[1] + poles[j, 1] * hat[0])
        return jnp.concatenate([right(left(basis_x, v), basis_y) for v in scaled], axis=0)

    @pl.loop(0, depth_count)
    def _(z):
        rowed = right(field[...].reshape(2 * nx, ny), basis_y)
        pl.when(z == 0)(forward_line)
        both = left(basis_x, beside([rowed[:nx], rowed[nx:]]))
        hat[0], hat[1] = both[:, :ny], both[:, ny:]
        pl.when(z == 0)(forward_across)

        for c in range(2):
            found = terms(c)
            if c == 0:
                pl.when(z == 0)(wait_partner)
                for d in range(n):
                    slow[d * rows:(d + 1) * rows, :] = bin_value / vall[d, z].astype(F32)
            total = found[(power_count - 1) * nx:]
            for j in range(power_count - 2, -1, -1):
                total = total * slow[...] + found[j * nx:(j + 1) * nx]
            field[c] = total

            if c == 0:
                for d in range(n):
                    mine[z, d % 2, d // 2] = field[0, d * rows:(d + 1) * rows, :]
                x_copy(z).start()
        pass_on(z)

    @pl.loop(0, depth_count)
    def _(z):
        irecv[z, lax.div(me, 2)] = part[z, lax.div(me, 2)]
        peers(half, 2, lambda p: i_copy(z, p, lax.div(p, 2)).wait_recv())
        total = irecv[z, 0]
        for i in range(1, half):
            total = total + irecv[z, i]
        image[z] = total

    peers(n, 1, lambda p: v_copy(p, p, me).wait_send())
    peers(n, 1, lambda p: p_copy(p, p, me).wait_send())
    peers(line, 4, lambda p: a_copy(p, me).wait_send())

    @pl.loop(0, half)
    def _(k):
        block = lax.rem(me + 2 * k, n)
        forward(vsel, block)[1].wait_send()

    @pl.loop(0, line)
    def _(k):
        block = lax.rem(me + 4 * k, n)
        forward(vsel, block)[0].wait_send()

    @pl.loop(0, depth_count)
    def _(z):
        x_copy(z).wait_send()
        peers(half, 2, lambda p: i_copy(z, p, lax.div(me, 2)).wait_send())


def on_device(n, traces, velocity, poly_coef, freq_slot, depth_owner):
    rows, ny, sample_count = traces.shape
    nx = velocity.shape[1]
    depth_count = depth_owner.shape[0]
    power_count = poly_coef.shape[2]
    assert freq_slot.shape[0] == n and velocity.shape[0] == 1 and n % 4 == 0
    sample_index = jnp.arange(sample_count, dtype=jnp.int32)
    phase_int = (freq_slot + 1)[:, None] * sample_index[None, :] % sample_count
    phases = phase_int.astype(F32) * (2.0 * math.pi / sample_count)
    dft_table = (jnp.stack([jnp.cos(phases), -jnp.sin(phases)]) / math.sqrt(sample_count)).astype(BF16)
    dft_table = dft_table * jnp.asarray(0.5, BF16)
    spectra = jnp.einsum("cft,xyt->fcxy", dft_table, traces, preferred_element_type=F32).astype(BF16)

    basis_x, eig_x = sine_basis(nx)
    basis_y, eig_y = sine_basis(ny)
    lam = jnp.asarray((np.outer(eig_x, eig_y) / 8.0 - 1.0).astype(np.float32))
    vmem = pl.BlockSpec(memory_space=pltpu.VMEM)
    smem = pl.BlockSpec(memory_space=pltpu.SMEM)
    half = n // 2
    dma = pltpu.SemaphoreType.DMA
    return pl.pallas_call(
        functools.partial(kernel, n),
        out_shape=(jax.ShapeDtypeStruct((depth_count, rows, ny), F32),
                   jax.ShapeDtypeStruct((2, nx, ny), F32)),
        in_specs=[smem, smem, smem] + [vmem] * 5,
        out_specs=(vmem, vmem),
        scratch_shapes=[
            pltpu.VMEM((n, 2, rows, ny), BF16),
            pltpu.VMEM((n, rows, ny), BF16),
            pltpu.VMEM((depth_count, rows, ny), BF16),
            pltpu.VMEM((n, depth_count, rows, ny), BF16),
            pltpu.VMEM((power_count, 2, nx, ny), F32),
            pltpu.VMEM((2, nx, ny), F32),
            pltpu.VMEM((nx, ny), F32),
            pltpu.VMEM((depth_count, 2, half, rows, ny), F32),
            pltpu.VMEM((depth_count, half, rows, ny), F32),
            pltpu.VMEM((depth_count, half, rows, ny), F32),
            pltpu.VMEM((depth_count, half, rows, ny), F32),
            *[dma((n,))] * 8,
            dma((depth_count,)), dma((depth_count,)),
            dma((depth_count, half)), dma((depth_count, half)),
        ],
        compiler_params=pltpu.CompilerParams(collective_id=0, has_side_effects=True),
    )(poly_coef.transpose(0, 2, 1), depth_owner, freq_slot, spectra, velocity.reshape(n, rows, ny), lam,
      jnp.asarray(np_split(basis_x)), jnp.asarray(np_split(basis_y)))


def solution(mesh):
    def step(*args):
        depth_image, wavefield = on_device(mesh.shape["freq"], *args)
        scale = 2.0 / math.sqrt(mesh.shape["freq"])
        return depth_image * scale, 2.0 * wavefield[:, None]

    return jax.shard_map(
        step,
        mesh=mesh,
        in_specs=(
            P(("group", "freq"), None, None),
            P(("group", "freq"), None, None),
            P(),
            P(),
            P("group"),
        ),
        out_specs=(P(None, ("group", "freq"), None), P(None, ("group", "freq"), None, None)),
        check_vma=False,
    )
```

```python
import functools
import math

import jax
import jax.numpy as jnp
import numpy as np
from jax import lax
from jax.experimental import pallas as pl
from jax.experimental.pallas import tpu as pltpu
from jax.sharding import PartitionSpec as P

F32, BF16 = jnp.float32, jnp.bfloat16


def sine_basis(size):
    index = np.arange(1, size + 1, dtype=np.float64)
    basis = math.sqrt(2.0 / (size + 1)) * np.sin(np.pi * np.outer(index, index) / (size + 1))
    return basis, 2.0 + 2.0 * np.cos(np.pi * index / (size + 1))


def split(values):
    high = values.astype(BF16)
    return high, (values - high.astype(F32)).astype(BF16)


def np_split(values):
    high = values.astype(BF16)
    return np.stack([high, (values - high.astype(np.float64)).astype(BF16)])


def dot(a, b):
    return lax.dot_general(a, b, (((1,), (0,)), ((), ())), preferred_element_type=F32)


def right(values, basis):
    high, low = split(values)
    return dot(high, basis[0]) + dot(low, basis[0]) + dot(high, basis[1])


def left(basis, values):
    high, low = split(values)
    return dot(basis[0], high) + dot(basis[0], low) + dot(basis[1], high)


def kernel(n, poly, owner, slot, spec, vel, lam, sx, sy, image, field,
           precv, vrecv, vsel, vall, poles, hat, slow, mine, theirs, part, cross, done, irecv,
           p_send, p_recv, w_send, w_recv, a_send, f_send, a_recv, g_send, x_send, x_recv, y_send, y_recv, i_send, i_recv):
    me = lax.axis_index("freq")
    core = lax.rem(me, 2)
    partner = me + 1 - 2 * core
    half, line = n // 2, n // 4
    across = me + 2 - 4 * lax.rem(lax.div(me, 2), 2)
    rows = spec.shape[2]
    nx, ny = field.shape[1:]
    depth_count = image.shape[0]
    power_count, term_count = poly.shape[1], poly.shape[2]

    def copy(src, dst, ssem, rsem, peer):
        return pltpu.make_async_remote_copy(
            src_ref=src, dst_ref=dst, send_sem=ssem, recv_sem=rsem,
            device_id={"freq": peer}, device_id_type=pl.DeviceIdType.MESH)

    def peers(count, step, body):
        @pl.loop(1, count)
        def _(k):
            body(lax.rem(me + step * k, n))

    barrier = pltpu.get_barrier_semaphore()
    peers(n, 1, lambda p: pl.semaphore_signal(
        barrier, inc=1, device_id={"freq": p}, device_id_type=pl.DeviceIdType.MESH))
    pl.semaphore_wait(barrier, n - 1)

    def v_copy(p, block, slot_of):
        return copy(vel.at[block], vrecv.at[slot_of], w_send.at[p], w_recv.at[slot_of], p)

    def p_copy(p, block, slot_of):
        return copy(spec.at[block], precv.at[slot_of], p_send.at[p], p_recv.at[slot_of], p)

    peers(n, 1, lambda p: v_copy(p, p, me).start())
    peers(n, 1, lambda p: p_copy(p, p, me).start())
    vrecv[me] = vel[me]
    precv[me] = spec[me]

    chunk = 16 if nx % 16 == 0 else nx

    @pl.loop(0, nx // chunk)
    def _(c):
        at = pl.ds(pl.multiple_of(c * chunk, chunk), chunk)
        x = lam[at, :]
        before, now = jnp.ones_like(x), x
        sums = [[jnp.full_like(x, poly[part_, j, 0]) + poly[part_, j, 1] * x for j in range(power_count)]
                for part_ in range(2)]
        for k in range(2, term_count):
            before, now = now, 2.0 * (x * now) - before
            for part_ in range(2):
                for j in range(power_count):
                    sums[part_][j] = sums[part_][j] + poly[part_, j, k] * now
        for part_ in range(2):
            for j in range(power_count):
                poles[j, part_, at, :] = sums[part_][j]

    peers(n, 1, lambda p: v_copy(p, p, p).wait_recv())
    for z in range(depth_count):
        vsel[z] = vrecv[owner[z]]
    vall[me] = vsel[...]

    def a_copy(p, slot_of):
        return copy(vsel, vall.at[slot_of], a_send.at[p], a_recv.at[slot_of], p)

    def forward(src, block):
        return (copy(src, vall.at[block], g_send.at[block], a_recv.at[block], across),
                copy(src, vall.at[block], f_send.at[block], a_recv.at[block], partner))

    peers(line, 4, lambda p: a_copy(p, me).start())
    for send in forward(vsel, me):
        send.start()

    peers(n, 1, lambda p: p_copy(p, p, p).wait_recv())
    for d in range(n):
        for c in range(2):
            field[c, d * rows:(d + 1) * rows, :] = precv[d, c].astype(F32)

    def forward_line():
        def body(p):
            a_copy(p, p).wait_recv()
            for send in forward(vall.at[p], p):
                send.start()

        peers(line, 4, body)

    def forward_across():
        @pl.loop(0, line)
        def _(k):
            block = lax.rem(across + 4 * k, n)
            a_copy(block, block).wait_recv()
            forward(vall.at[block], block)[1].start()

    def wait_partner():
        @pl.loop(0, half)
        def _(k):
            block = lax.rem(partner + 2 * k, n)
            a_copy(block, block).wait_recv()

    bin_value = (slot[me] + 1).astype(F32) * (1.0 / n)

    def x_copy(z):
        return copy(mine.at[z, 1 - core], theirs.at[z], x_send.at[z], x_recv.at[z], partner)

    side, place = lax.rem(lax.div(me, 2), 2), lax.div(me, 4)

    def y_copy(z):
        return copy(part.at[z, 1 - side], cross.at[z], y_send.at[z], y_recv.at[z], across)

    def i_copy(z, p, slot_of):
        return copy(done.at[z, lax.div(p, 4)], irecv.at[z, slot_of],
                    i_send.at[z, lax.div(p, 4)], i_recv.at[z, slot_of], p)

    def pass_across(z):
        x_copy(z).wait_recv()
        part[z] = mine[z, core] + theirs[z]
        y_copy(z).start()

    def pass_line(z):
        y_copy(z).wait_recv()
        done[z] = part[z, side] + cross[z]
        peers(line, 4, lambda p: i_copy(z, p, place).start())

    sxh, sxl, syh, syl = sx[0], sx[1], sy[0], sy[1]
    basis_x, basis_y = (sxh, sxl), (syh, syl)

    def beside(blocks):
        return jnp.concatenate(blocks, axis=1)

    def below(values, count):
        width = values.shape[1] // count
        return jnp.concatenate([values[:, i * width:(i + 1) * width] for i in range(count)], axis=0)

    def terms(c):
        scaled = []
        for j in range(power_count):
            if c == 0:
                scaled.append(poles[j, 0] * hat[0] - poles[j, 1] * hat[1])
            else:
                scaled.append(poles[j, 0] * hat[1] + poles[j, 1] * hat[0])
        return jnp.concatenate([right(left(basis_x, v), basis_y) for v in scaled], axis=0)

    @pl.loop(0, depth_count)
    def _(z):
        rowed = right(field[...].reshape(2 * nx, ny), basis_y)
        pl.when(z == 0)(forward_line)
        both = left(basis_x, beside([rowed[:nx], rowed[nx:]]))
        hat[0], hat[1] = both[:, :ny], both[:, ny:]
        pl.when(z == 0)(forward_across)

        for c in range(2):
            found = terms(c)
            if c == 0:
                pl.when(z > 0)(lambda: pass_line(z - 1))
                pl.when(z == 0)(wait_partner)
                for d in range(n):
                    slow[d * rows:(d + 1) * rows, :] = bin_value / vall[d, z].astype(F32)
            total = found[(power_count - 1) * nx:]
            for j in range(power_count - 2, -1, -1):
                total = total * slow[...] + found[j * nx:(j + 1) * nx]
            field[c] = total

            if c == 0:
                for d in range(n):
                    mine[z, d % 2, (d // 2) % 2, d // 4] = field[0, d * rows:(d + 1) * rows, :]
                x_copy(z).start()
        pass_across(z)

    pass_line(depth_count - 1)

    @pl.loop(0, depth_count)
    def _(z):
        irecv[z, place] = done[z, place]
        peers(line, 4, lambda p: i_copy(z, p, lax.div(p, 4)).wait_recv())
        total = irecv[z, 0]
        for i in range(1, line):
            total = total + irecv[z, i]
        image[z] = total

    peers(n, 1, lambda p: v_copy(p, p, me).wait_send())
    peers(n, 1, lambda p: p_copy(p, p, me).wait_send())
    peers(line, 4, lambda p: a_copy(p, me).wait_send())

    @pl.loop(0, half)
    def _(k):
        block = lax.rem(me + 2 * k, n)
        forward(vsel, block)[1].wait_send()

    @pl.loop(0, line)
    def _(k):
        block = lax.rem(me + 4 * k, n)
        forward(vsel, block)[0].wait_send()

    @pl.loop(0, depth_count)
    def _(z):
        x_copy(z).wait_send()
        y_copy(z).wait_send()
        peers(line, 4, lambda p: i_copy(z, p, place).wait_send())


def on_device(n, traces, velocity, poly_coef, freq_slot, depth_owner):
    rows, ny, sample_count = traces.shape
    nx = velocity.shape[1]
    depth_count = depth_owner.shape[0]
    power_count = poly_coef.shape[2]
    assert freq_slot.shape[0] == n and velocity.shape[0] == 1 and n % 4 == 0
    sample_index = jnp.arange(sample_count, dtype=jnp.int32)
    phase_int = (freq_slot + 1)[:, None] * sample_index[None, :] % sample_count
    phases = phase_int.astype(F32) * (2.0 * math.pi / sample_count)
    dft_table = (jnp.stack([jnp.cos(phases), -jnp.sin(phases)]) / math.sqrt(sample_count)).astype(BF16)
    dft_table = dft_table * jnp.asarray(0.5, BF16)
    spectra = jnp.einsum("cft,xyt->fcxy", dft_table, traces, preferred_element_type=F32).astype(BF16)

    basis_x, eig_x = sine_basis(nx)
    basis_y, eig_y = sine_basis(ny)
    lam = jnp.asarray((np.outer(eig_x, eig_y) / 8.0 - 1.0).astype(np.float32))
    vmem = pl.BlockSpec(memory_space=pltpu.VMEM)
    smem = pl.BlockSpec(memory_space=pltpu.SMEM)
    line = n // 4
    dma = pltpu.SemaphoreType.DMA
    return pl.pallas_call(
        functools.partial(kernel, n),
        out_shape=(jax.ShapeDtypeStruct((depth_count, rows, ny), F32),
                   jax.ShapeDtypeStruct((2, nx, ny), F32)),
        in_specs=[smem, smem, smem] + [vmem] * 5,
        out_specs=(vmem, vmem),
        scratch_shapes=[
            pltpu.VMEM((n, 2, rows, ny), BF16),
            pltpu.VMEM((n, rows, ny), BF16),
            pltpu.VMEM((depth_count, rows, ny), BF16),
            pltpu.VMEM((n, depth_count, rows, ny), BF16),
            pltpu.VMEM((power_count, 2, nx, ny), F32),
            pltpu.VMEM((2, nx, ny), F32),
            pltpu.VMEM((nx, ny), F32),
            pltpu.VMEM((depth_count, 2, 2, line, rows, ny), F32),
            pltpu.VMEM((depth_count, 2, line, rows, ny), F32),
            pltpu.VMEM((depth_count, 2, line, rows, ny), F32),
            pltpu.VMEM((depth_count, line, rows, ny), F32),
            pltpu.VMEM((depth_count, line, rows, ny), F32),
            pltpu.VMEM((depth_count, line, rows, ny), F32),
            *[dma((n,))] * 8,
            *[dma((depth_count,))] * 4,
            dma((depth_count, line)), dma((depth_count, line)),
        ],
        compiler_params=pltpu.CompilerParams(collective_id=0, has_side_effects=True),
    )(poly_coef.transpose(0, 2, 1), depth_owner, freq_slot, spectra, velocity.reshape(n, rows, ny), lam,
      jnp.asarray(np_split(basis_x)), jnp.asarray(np_split(basis_y)))


def solution(mesh):
    def step(*args):
        depth_image, wavefield = on_device(mesh.shape["freq"], *args)
        scale = 2.0 / math.sqrt(mesh.shape["freq"])
        return depth_image * scale, 2.0 * wavefield[:, None]

    return jax.shard_map(
        step,
        mesh=mesh,
        in_specs=(
            P(("group", "freq"), None, None),
            P(("group", "freq"), None, None),
            P(),
            P(),
            P("group"),
        ),
        out_specs=(P(None, ("group", "freq"), None), P(None, ("group", "freq"), None, None)),
        check_vma=False,
    )
```
